32 devices in a mesh: gx: 4 (over z), gy: 4 (over y, x), ma: 2 (over core).
Axes of the slice: x: 2, y: 2, z: 4, core: 2. Of those that a mesh axis runs over, the one named last changes fastest.
Arguments:
- perturbations: float32 [30, 2, 128, 2048], P('ma', None, 'gx', 'gy'), may hold values from -6 to 6
- coefficients: float32 [2, 128, 2048], P(None, 'gx', 'gy'), may hold values from 0.02 to 0.12
- coarse_coefficients: float32 [2, 32, 512], P(None, 'gx', 'gy'), may hold values from 0.02 to 0.12
- iterate: float32 [2, 128, 2048], P(None, 'gx', 'gy'), may hold values from -6 to 6
- residual: float32 [2, 128, 2048], P(None, 'gx', 'gy'), may hold values from -6 to 6
- direction: float32 [2, 128, 2048], P(None, 'gx', 'gy'), may hold values from -6 to 6
Outputs:
- new_iterate: float32 [2, 128, 2048], P(None, 'gx', 'gy')
- new_residual: float32 [2, 128, 2048], P(None, 'gx', 'gy')
- new_direction: float32 [2, 128, 2048], P(None, 'gx', 'gy')
The draws below stay inside these ranges and needn't reach their ends.
All inputs are finite; a program needn't handle non-finite values.
Results may differ from the reference program's by a relative error of at most 0.0001.
Values sent between devices are 32-bit elements; how exact they have to be, the bound alone decides.
A program may use at most 192 MiB of HBM per device.

```python
import jax
import jax.numpy as jnp
from jax import lax

MEMBERS = 30
LEV = 2
PASSES = 3
RATIO = 4
NX = 128
NY = 2048


def block_levels(rng, extent, shards, smallest, top_value):
    def one(axis_at, shards_of):
        steps = jax.random.uniform(jax.random.fold_in(jax.random.fold_in(rng, 6), axis_at), (shards_of,), jnp.float32, smallest / len(shards), top_value / len(shards))
        return jnp.repeat(jnp.exp(steps), extent[axis_at] // shards_of).reshape((-1,) + (1,) * (len(extent) - axis_at - 1))

    level = one(*shards[0])
    for cut in shards[1:]:
        level = level * one(*cut)
    return level


def scatter_about(stream_key, extent, spread, reach, shards=(), kind=jnp.bfloat16):
    values = jax.random.normal(stream_key, extent, jnp.float32) * spread
    if len(shards) > 0:
        values = block_levels(stream_key, extent, shards, -0.22, 0.18) * values
    return jnp.clip(values, min=-reach, max=reach).astype(kind)


def setup_inputs(seed: int = 0) -> dict:
    key_of = jax.random.split(jax.random.key(seed), 7)
    perturbations = scatter_about(key_of[0], (MEMBERS, LEV, NX, NY), 1.0, 6.0, ((0, 2), (2, 4), (3, 4)), jnp.float32)
    coefficients = jnp.clip(0.02 + 0.09999999776482582 * jax.random.uniform(key_of[1], (2, NX, NY), jnp.float32) ** block_levels(key_of[1], (2, NX, NY), ((1, 4), (2, 4)), -0.2, 0.2), 0.02, 0.12)
    coarse_coefficients = jnp.clip(0.02 + 0.09999999776482582 * jax.random.uniform(key_of[2], (2, NX // RATIO, NY // RATIO), jnp.float32) ** block_levels(key_of[2], (2, NX // RATIO, NY // RATIO), ((1, 4), (2, 4)), -0.2, 0.2), 0.02, 0.12)
    iterate = scatter_about(key_of[3], (LEV, NX, NY), 1.0, 6.0, ((1, 4), (2, 4)), jnp.float32)
    residual = scatter_about(key_of[4], (LEV, NX, NY), 1.0, 6.0, ((1, 4), (2, 4)), jnp.float32)
    direction = scatter_about(key_of[5], (LEV, NX, NY), 1.0, 6.0, ((1, 4), (2, 4)), jnp.float32)
    return {"perturbations": perturbations, "coefficients": coefficients, "coarse_coefficients": coarse_coefficients, "iterate": iterate, "residual": residual, "direction": direction}


def stencil_pass(source, coef_x, coef_y):
    centre = source[..., 1:-1, 1:-1]
    edge_x = 0.5 * (coef_x[1:, 1:-1] + coef_x[:-1, 1:-1])
    edge_y = 0.5 * (coef_y[1:-1, 1:] + coef_y[1:-1, :-1])
    along_x = edge_x[1:] * (source[..., 2:, 1:-1] - centre) - edge_x[:-1] * (centre - source[..., :-2, 1:-1])
    along_y = edge_y[:, 1:] * (source[..., 1:-1, 2:] - centre) - edge_y[:, :-1] * (centre - source[..., 1:-1, :-2])
    return centre + along_x + along_y


def smooth_level(source, coefficient_pair):
    padding = [(0, 0)] * (source.ndim - 2) + [(1, 1), (1, 1)]
    padded_coefs = jnp.pad(coefficient_pair, ((0, 0), (1, 1), (1, 1)))
    result = source
    for sweep_index in range(PASSES):
        result = stencil_pass(jnp.pad(result, padding), padded_coefs[0], padded_coefs[1])
    return result


def restrict_blocks(source):
    shaped = source.reshape(source.shape[:-2] + (source.shape[-2] // RATIO, RATIO, source.shape[-1] // RATIO, RATIO))
    return jnp.mean(shaped, axis=(-3, -1))


def prolong_blocks(source):
    return jnp.repeat(jnp.repeat(source, RATIO, axis=-2), RATIO, axis=-1)


def reference(perturbations, coefficients, coarse_coefficients, iterate, residual, direction):
    def add_member(running_sum, member):
        weighted = member * direction
        fine_part = smooth_level(weighted, coefficients)
        coarse_part = smooth_level(restrict_blocks(weighted), coarse_coefficients)
        localized = fine_part + prolong_blocks(coarse_part)
        return running_sum + member * localized, None

    running_sum, unused = lax.scan(add_member, jnp.zeros_like(direction), perturbations)
    operator_image = direction + running_sum / (MEMBERS - 1)
    norm_old = jnp.sum(residual * residual)
    step_length = norm_old / jnp.sum(direction * operator_image)
    new_iterate = iterate + step_length * direction
    new_residual = residual - step_length * operator_image
    norm_new = jnp.sum(new_residual * new_residual)
    new_direction = new_residual + (norm_new / norm_old) * direction
    return (new_iterate, new_residual, new_direction)
```

```python
import functools

import jax
import jax.numpy as jnp
from jax import lax
from jax.experimental import pallas as pl
from jax.experimental.pallas import tpu as pltpu
from jax.sharding import PartitionSpec as P

MEMBERS = 30
PASSES = 3
RATIO = 4
HALO = 4
LANES = 128
CHUNKS = 4
MESH = pl.DeviceIdType.MESH
F32 = jnp.float32
BF16 = jnp.bfloat16


def shift_up(u, axis):
    return pltpu.roll(u, u.shape[axis] - 1, axis)


def shift_down(u, axis):
    return pltpu.roll(u, 1, axis)


def split_dot(a, b):
    high = a.astype(BF16)
    low = (a - high.astype(F32)).astype(BF16)
    return jnp.dot(high, b, preferred_element_type=F32) + jnp.dot(
        low, b, preferred_element_type=F32
    )


def stencil_weights(cx, cy, rows, cols, has_prev, has_next, has_left, has_right):
    ext_rows, ext_cols = cx.shape
    row = lax.broadcasted_iota(jnp.int32, (ext_rows, ext_cols), 0)
    col = lax.broadcasted_iota(jnp.int32, (ext_rows, ext_cols), 1)
    outside = (
        ((row >= rows) & (row < rows + HALO) & (has_next == 0))
        | ((row >= rows + HALO) & (has_prev == 0))
        | ((col >= cols) & (col < cols + LANES // 2) & (has_right == 0))
        | ((col >= cols + LANES // 2) & (has_left == 0))
    )
    xp = 0.5 * (cx + shift_up(cx, 0))
    xm = shift_down(xp, 0)
    yp = 0.5 * (cy + shift_up(cy, 1))
    ym = shift_down(yp, 1)
    centre = 1.0 - xp - xm - yp - ym
    return [jnp.where(outside, 0.0, value) for value in (centre, xp, xm, yp, ym)]


def apply_passes(u, weights):
    for _ in range(PASSES):
        u = (
            weights[0][...] * u
            + weights[1][...] * shift_up(u, 0)
            + weights[2][...] * shift_down(u, 0)
            + weights[3][...] * shift_up(u, 1)
            + weights[4][...] * shift_down(u, 1)
        )
    return u


def kernel(
    sizes,
    p_ref, coef_ref, ccoef_ref, r_ref, d_ref,
    q_ref, sums_ref,
    wf, wc, line, lanes_out,
    x_top, x_bottom, c_top, c_bottom, strips,
    rx_next, rx_prev, rc_next, rc_prev, ry, rd,
    hy, hyc, fine_weights, coarse_weights,
    acc, acc_other, part, slots,
    send_sem, recv_sem, group_send, group_recv,
):
    n_x, n_y = sizes
    half, levels, rows, cols = p_ref.shape
    crows, ccols = ccoef_ref.shape[1], ccoef_ref.shape[2]
    gx, gy, ma = lax.axis_index("gx"), lax.axis_index("gy"), lax.axis_index("ma")
    me = gx * n_y + gy
    group = n_x * n_y
    has = {
        (-1, 0): gx > 0, (1, 0): gx < n_x - 1, (0, -1): gy > 0, (0, 1): gy < n_y - 1,
    }
    for dx in (-1, 1):
        for dy in (-1, 1):
            has[(dx, dy)] = has[(dx, 0)] & has[(0, dy)]

    barrier = pltpu.get_barrier_semaphore()

    def greet(k, carry):
        @pl.when(k != me)
        def _():
            pl.semaphore_signal(
                barrier, inc=1, device_id={"gx": k // n_y, "gy": k % n_y}, device_id_type=MESH
            )
        return carry

    lax.fori_loop(0, group, greet, 0)
    pl.semaphore_signal(barrier, inc=1, device_id={"ma": 1 - ma}, device_id_type=MESH)

    def zero_if(absent, ref):
        @pl.when(absent)
        def _():
            ref[...] = jnp.zeros_like(ref)

    zero_if(gx == 0, rx_prev)
    zero_if(gx == 0, rc_prev)
    zero_if(gx == n_x - 1, rx_next)
    zero_if(gx == n_x - 1, rc_next)
    for side in (0, 1):
        dy = 2 * side - 1
        zero_if(jnp.logical_not(has[(0, dy)]), ry.at[side])
        for way in (0, 1):
            zero_if(jnp.logical_not(has[(2 * way - 1, dy)]), rd.at[side, way])

    def weigh(m, carry):
        w = p_ref[m] * d_ref[...]
        wf[m] = w
        x_top[m] = w[:, :HALO]
        x_bottom[m] = w[:, rows - HALO :]
        return carry

    coefs = coef_ref[...]
    wf[half] = coefs
    x_top[half] = coefs[:, :HALO]
    x_bottom[half] = coefs[:, rows - HALO :]
    lax.fori_loop(0, half, weigh, 0)

    pl.semaphore_wait(barrier, group)

    moves = []

    def move(src, dst, dx, dy):
        slot = len(moves)
        target = {
            "gx": jnp.clip(gx + dx, 0, n_x - 1) if dx else gx,
            "gy": jnp.clip(gy + dy, 0, n_y - 1) if dy else gy,
        }
        copy = pltpu.make_async_remote_copy(
            src_ref=src, dst_ref=dst, send_sem=send_sem.at[slot], recv_sem=recv_sem.at[slot],
            device_id=target, device_id_type=MESH,
        )
        moves.append((copy, has[(dx, dy)], has[(-dx, -dy)]))

        @pl.when(has[(dx, dy)])
        def _():
            copy.start()

        return slot

    def arrive(slot):
        @pl.when(moves[slot][2])
        def _():
            moves[slot][0].wait_recv()

    total = half + 1
    bounds = [total - (total * k) // CHUNKS for k in range(CHUNKS + 1)]
    x_moves = []
    for k in range(CHUNKS):
        low, high = bounds[k + 1], bounds[k]
        span = pl.ds(low, high - low)
        x_moves.append(
            (
                move(x_top.at[span], rx_next.at[span], -1, 0),
                move(x_bottom.at[span], rx_prev.at[span], 1, 0),
                low, high,
            )
        )

    pick = lax.broadcasted_iota(jnp.int32, (cols, ccols), 0) // RATIO
    gather = jnp.where(
        pick == lax.broadcasted_iota(jnp.int32, (cols, ccols), 1), 1.0 / RATIO**2, 0.0
    ).astype(BF16)

    def restrict(m, carry):
        values = wf[m].reshape(levels * rows, cols)
        line[pl.ds(pl.multiple_of(m * levels * rows, 8), levels * rows)] = split_dot(values, gather)
        return carry

    lax.fori_loop(0, half, restrict, 0)
    count = half * levels * crows
    coarse = line[pl.ds(0, count, stride=RATIO), :]
    for k in range(1, RATIO):
        coarse = coarse + line[pl.ds(k, count, stride=RATIO), :]
    wc[pl.ds(0, half)] = coarse.reshape(half, levels, crows, ccols)
    wc[half] = ccoef_ref[...]
    every = wc[...]
    c_top[...] = every[:, :, :HALO]
    c_bottom[...] = every[:, :, crows - HALO :]
    c_moves = [move(c_top, rc_next, -1, 0), move(c_bottom, rc_prev, 1, 0)]

    flane = lax.broadcasted_iota(jnp.int32, (rows, LANES), 1)
    clane = lax.broadcasted_iota(jnp.int32, (crows, LANES), 1)

    def pack(m, carry):
        fl, fr, cl, cr = carry
        for level in range(levels):
            at = PASSES * (m * levels + level)
            fmask = (flane >= at) & (flane < at + PASSES)
            cmask = (clane >= at) & (clane < at + PASSES)
            fl = jnp.where(fmask, pltpu.roll(wf[m, level, :, :LANES], at, 1), fl)
            fr = jnp.where(fmask, pltpu.roll(wf[m, level, :, cols - LANES :], at + PASSES, 1), fr)
            field = wc[m, level]
            cl = jnp.where(cmask, pltpu.roll(field[:, :LANES], at, 1), cl)
            cr = jnp.where(cmask, pltpu.roll(field[:, ccols - LANES :], at + PASSES, 1), cr)
        return fl, fr, cl, cr

    fzero = jnp.zeros((rows, LANES), F32)
    czero = jnp.zeros((crows, LANES), F32)
    fl, fr, cl, cr = lax.fori_loop(0, total, pack, (fzero, fzero, czero, czero))
    for side, (fine, small) in enumerate(((fl, cl), (fr, cr))):
        strips[side, 0:crows] = small
        strips[side, crows : crows + rows] = fine
        strips[side, crows + rows :] = small
    y_moves = []
    for side in (0, 1):
        dy = 2 * side - 1
        other = 1 - side
        y_moves.append(move(strips.at[side, pl.ds(0, crows + rows)], ry.at[other], 0, dy))
        y_moves.append(move(strips.at[side, pl.ds(0, 16)], rd.at[other, 1], -1, dy))
        y_moves.append(move(strips.at[side, pl.ds(crows + rows - 8, 16)], rd.at[other, 0], 1, dy))

    for slot in y_moves:
        arrive(slot)
    for slot in c_moves:
        arrive(slot)

    near = lax.broadcasted_iota(jnp.int32, (8, LANES), 0) < HALO
    for side in (0, 1):
        hyc[side, 0:crows] = ry[side, 0:crows]
        hyc[side, crows : crows + 8] = jnp.where(near, rd[side, 1, 0:8], rd[side, 0, 8:16])
        hy[side, 0:rows] = ry[side, crows : crows + rows]
        hy[side, rows : rows + 8] = jnp.where(near, rd[side, 1, 8:16], rd[side, 0, 0:8])

    def columns(ref, index, height):
        lane = lax.broadcasted_iota(jnp.int32, (height, LANES), 1)
        at = PASSES * index
        right = pltpu.roll(ref[1], LANES - at, 1)
        left = pltpu.roll(ref[0], LANES - PASSES - at, 1)
        return jnp.where(
            lane < PASSES, right, jnp.where(lane >= LANES - PASSES, left, 0.0)
        )

    def extended(main, nxt, prv, ref, index):
        height = main.shape[0] + 2 * HALO
        tall = jnp.concatenate([main, jnp.concatenate([nxt, prv], axis=0)], axis=0)
        return jnp.concatenate([tall, columns(ref, index, height)], axis=1)

    def coarse_field(m, level):
        return extended(
            wc[m, level], rc_next[m, level], rc_prev[m, level], hyc, m * levels + level
        )

    def fine_field(m, level):
        return extended(
            wf[m, level], rx_next[m, level], rx_prev[m, level], hy, m * levels + level
        )

    ends = [
        value.astype(jnp.int32)
        for value in (has[(-1, 0)], has[(1, 0)], has[(0, -1)], has[(0, 1)])
    ]
    for k, value in enumerate(
        stencil_weights(coarse_field(half, 0), coarse_field(half, 1), crows, ccols, *ends)
    ):
        coarse_weights[k] = value

    spread = jnp.where(
        lax.broadcasted_iota(jnp.int32, (ccols, cols), 1) // RATIO
        == lax.broadcasted_iota(jnp.int32, (ccols, cols), 0),
        1.0, 0.0,
    ).astype(BF16)

    def coarse_member(m, carry):
        for level in range(levels):
            u = apply_passes(coarse_field(m, level), [coarse_weights.at[k] for k in range(5)])
            start = pl.multiple_of((m * levels + level) * crows, 8)
            wc[m, level] = u[:crows, :ccols]
        return carry

    lax.fori_loop(0, half, coarse_member, 0)
    lanes_out[...] = split_dot(
        wc[pl.ds(0, half)].reshape(half * levels * crows, ccols), spread
    )

    acc[...] = jnp.zeros_like(acc)
    upper = lax.broadcasted_iota(jnp.int32, (2 * RATIO, cols), 0) < RATIO

    def fine_member(m, carry):
        for level in range(levels):
            u = apply_passes(fine_field(m, level), [fine_weights.at[k] for k in range(5)])
            u = u[:rows, :cols]
            base = (m * levels + level) * crows
            for t in range(rows // (2 * RATIO)):
                a = jnp.broadcast_to(lanes_out[pl.ds(base + 2 * t, 1), :], (2 * RATIO, cols))
                b = jnp.broadcast_to(lanes_out[pl.ds(base + 2 * t + 1, 1), :], (2 * RATIO, cols))
                at = slice(2 * RATIO * t, 2 * RATIO * (t + 1))
                acc[level, at] += p_ref[m, level, at] * (u[at] + jnp.where(upper, a, b))
        return carry

    for k, (first, second, low, high) in enumerate(x_moves):
        arrive(first)
        arrive(second)
        if k == 0:
            for j, value in enumerate(
                stencil_weights(fine_field(half, 0), fine_field(half, 1), rows, cols, *ends)
            ):
                fine_weights[j] = value
        lax.fori_loop(low, min(high, half), fine_member, 0)

    swap = pltpu.make_async_remote_copy(
        src_ref=acc, dst_ref=acc_other, send_sem=send_sem.at[len(moves)],
        recv_sem=recv_sem.at[len(moves)], device_id={"ma": 1 - ma}, device_id_type=MESH,
    )
    swap.start()
    swap.wait_recv()
    d, r = d_ref[...], r_ref[...]
    q = d + (acc[...] + acc_other[...]) / (MEMBERS - 1)
    q_ref[...] = q

    def total_row(value):
        flat = value.reshape(levels * rows // 8, 8, cols)
        tile = jnp.sum(flat, axis=0)
        narrow = tile[:, :LANES]
        for k in range(1, cols // LANES):
            narrow = narrow + tile[:, k * LANES : (k + 1) * LANES]
        return jnp.sum(narrow, axis=0, keepdims=True)

    row = lax.broadcasted_iota(jnp.int32, (8, LANES), 0)
    packed = jnp.zeros((8, LANES), F32)
    for k, value in enumerate((r * r, d * q, r * q, q * q)):
        packed = jnp.where(row == k, total_row(value), packed)
    part[...] = packed
    slots[me] = packed

    def to_peer(k):
        return pltpu.make_async_remote_copy(
            src_ref=part, dst_ref=slots.at[me], send_sem=group_send.at[k],
            recv_sem=group_recv.at[me],
            device_id={"gx": k // n_y, "gy": k % n_y}, device_id_type=MESH,
        )

    def from_peer(k):
        return pltpu.make_async_remote_copy(
            src_ref=part, dst_ref=slots.at[k], send_sem=group_send.at[k],
            recv_sem=group_recv.at[k],
            device_id={"gx": k // n_y, "gy": k % n_y}, device_id_type=MESH,
        )

    def each_peer(action):
        def body(k, carry):
            @pl.when(k != me)
            def _():
                action(k)
            return carry

        lax.fori_loop(0, group, body, 0)

    each_peer(lambda k: to_peer(k).start())
    each_peer(lambda k: from_peer(k).wait_recv())
    summed = jnp.sum(slots[...], axis=0)
    sums_ref[...] = jnp.broadcast_to(jnp.sum(summed, axis=1, keepdims=True), (8, LANES))

    each_peer(lambda k: to_peer(k).wait_send())
    swap.wait_send()
    for copy, sends, _ in moves:
        @pl.when(sends)
        def _():
            copy.wait_send()


def local(n_x, n_y, perturbations, coefficients, coarse_coefficients, iterate, residual, direction):
    half, levels, rows, cols = perturbations.shape
    _, crows, ccols = coarse_coefficients.shape
    total = half + 1
    group = n_x * n_y
    n_moves = 2 * CHUNKS + 2 + 6 + 1
    vmem = pl.BlockSpec(memory_space=pltpu.VMEM)
    q, sums = pl.pallas_call(
        functools.partial(kernel, (n_x, n_y)),
        out_shape=(
            jax.ShapeDtypeStruct((levels, rows, cols), F32),
            jax.ShapeDtypeStruct((8, LANES), F32),
        ),
        in_specs=[vmem] * 5,
        out_specs=(vmem, vmem),
        scratch_shapes=[
            pltpu.VMEM((total, levels, rows, cols), F32),
            pltpu.VMEM((total, levels, crows, ccols), F32),
            pltpu.VMEM((half * levels * rows, ccols), F32),
            pltpu.VMEM((half * levels * crows, cols), F32),
            pltpu.VMEM((total, levels, HALO, cols), F32),
            pltpu.VMEM((total, levels, HALO, cols), F32),
            pltpu.VMEM((total, levels, HALO, ccols), F32),
            pltpu.VMEM((total, levels, HALO, ccols), F32),
            pltpu.VMEM((2, rows + 2 * crows, LANES), F32),
            pltpu.VMEM((total, levels, HALO, cols), F32),
            pltpu.VMEM((total, levels, HALO, cols), F32),
            pltpu.VMEM((total, levels, HALO, ccols), F32),
            pltpu.VMEM((total, levels, HALO, ccols), F32),
            pltpu.VMEM((2, rows + crows, LANES), F32),
            pltpu.VMEM((2, 2, 16, LANES), F32),
            pltpu.VMEM((2, rows + 2 * HALO, LANES), F32),
            pltpu.VMEM((2, crows + 2 * HALO, LANES), F32),
            pltpu.VMEM((5, rows + 2 * HALO, cols + LANES), F32),
            pltpu.VMEM((5, crows + 2 * HALO, ccols + LANES), F32),
            pltpu.VMEM((levels, rows, cols), F32),
            pltpu.VMEM((levels, rows, cols), F32),
            pltpu.VMEM((8, LANES), F32),
            pltpu.VMEM((group, 8, LANES), F32),
            pltpu.SemaphoreType.DMA((n_moves,)),
            pltpu.SemaphoreType.DMA((n_moves,)),
            pltpu.SemaphoreType.DMA((group,)),
            pltpu.SemaphoreType.DMA((group,)),
        ],
        compiler_params=pltpu.CompilerParams(
            collective_id=0, has_side_effects=True, vmem_limit_bytes=48 << 20
        ),
    )(perturbations, coefficients, coarse_coefficients, residual, direction)
    norm_old, curvature, cross, image = (sums[k, 0] for k in range(4))
    step_length = norm_old / curvature
    norm_new = norm_old + step_length * (step_length * image - 2.0 * cross)
    new_iterate = iterate + step_length * direction
    new_residual = residual - step_length * q
    new_direction = new_residual + norm_new / norm_old * direction
    return (new_iterate, new_residual, new_direction)


def solution(mesh):
    cell = P(None, "gx", "gy")
    return jax.shard_map(
        functools.partial(local, mesh.shape["gx"], mesh.shape["gy"]),
        mesh=mesh,
        in_specs=(P("ma", None, "gx", "gy"), cell, cell, cell, cell, cell),
        out_specs=(cell, cell, cell),
        check_vma=False,
    )
```

```python
import functools

import jax
import jax.numpy as jnp
from jax import lax
from jax.experimental import pallas as pl
from jax.experimental.pallas import tpu as pltpu
from jax.sharding import PartitionSpec as P

MEMBERS = 30
PASSES = 3
RATIO = 4
HALO = 4
LANES = 128
CHUNKS = 4
MESH = pl.DeviceIdType.MESH
F32 = jnp.float32
BF16 = jnp.bfloat16


def shift_up(u, axis):
    return pltpu.roll(u, u.shape[axis] - 1, axis)


def shift_down(u, axis):
    return pltpu.roll(u, 1, axis)


def split_dot(a, b):
    high = a.astype(BF16)
    low = (a - high.astype(F32)).astype(BF16)
    return jnp.dot(high, b, preferred_element_type=F32) + jnp.dot(
        low, b, preferred_element_type=F32
    )


def stencil_weights(cx, cy, rows, cols, has_prev, has_next, has_left, has_right):
    ext_rows, ext_cols = cx.shape
    row = lax.broadcasted_iota(jnp.int32, (ext_rows, ext_cols), 0)
    col = lax.broadcasted_iota(jnp.int32, (ext_rows, ext_cols), 1)
    outside = (
        ((row >= rows) & (row < rows + HALO) & (has_next == 0))
        | ((row >= rows + HALO) & (has_prev == 0))
        | ((col >= cols) & (col < cols + LANES // 2) & (has_right == 0))
        | ((col >= cols + LANES // 2) & (has_left == 0))
    )
    xp = 0.5 * (cx + shift_up(cx, 0))
    xm = shift_down(xp, 0)
    yp = 0.5 * (cy + shift_up(cy, 1))
    ym = shift_down(yp, 1)
    centre = 1.0 - xp - xm - yp - ym
    return [jnp.where(outside, 0.0, value) for value in (centre, xp, xm, yp, ym)]


def apply_passes(u, weights):
    for _ in range(PASSES):
        u = (
            weights[0][...] * u
            + weights[1][...] * shift_up(u, 0)
            + weights[2][...] * shift_down(u, 0)
            + weights[3][...] * shift_up(u, 1)
            + weights[4][...] * shift_down(u, 1)
        )
    return u


def kernel(
    sizes,
    p_hbm, coef_hbm, ccoef_hbm, r_hbm, d_hbm,
    q_ref, step_ref, growth_ref,
    p_ref, coef_ref, ccoef_ref, r_ref, d_ref,
    wc, line, lanes_out,
    x_top, x_bottom, c_top, c_bottom, strips,
    rx_next, rx_prev, rc_next, rc_prev, ry, rd,
    hy, hyc, fine_weights, coarse_weights,
    acc, acc_other, part, slots,
    load_sem, send_sem, recv_sem, group_send, group_recv,
):
    n_x, n_y = sizes
    half, levels, rows, cols = p_ref.shape
    crows, ccols = ccoef_ref.shape[1], ccoef_ref.shape[2]
    gx, gy, ma = lax.axis_index("gx"), lax.axis_index("gy"), lax.axis_index("ma")
    me = gx * n_y + gy
    group = n_x * n_y
    has = {
        (-1, 0): gx > 0, (1, 0): gx < n_x - 1, (0, -1): gy > 0, (0, 1): gy < n_y - 1,
    }
    for dx in (-1, 1):
        for dy in (-1, 1):
            has[(dx, dy)] = has[(dx, 0)] & has[(0, dy)]

    def each_peer(action):
        def body(step, carry):
            action(lax.rem(me + step, group))
            return carry

        lax.fori_loop(1, group, body, 0, unroll=group <= 16)

    barrier = pltpu.get_barrier_semaphore()
    pl.semaphore_signal(barrier, inc=1, device_id={"ma": 1 - ma}, device_id_type=MESH)
    each_peer(
        lambda k: pl.semaphore_signal(
            barrier, inc=1, device_id={"gx": k // n_y, "gy": k % n_y}, device_id_type=MESH
        )
    )

    total = half + 1
    bounds = [total - (total * k) // CHUNKS for k in range(CHUNKS + 1)]
    loads = [
        pltpu.make_async_copy(src, dst, load_sem.at[k])
        for k, (src, dst) in enumerate(
            ((d_hbm, d_ref), (coef_hbm, coef_ref), (ccoef_hbm, ccoef_ref), (r_hbm, r_ref))
        )
    ]
    for k in range(CHUNKS):
        span = pl.ds(bounds[k + 1], min(bounds[k], half) - bounds[k + 1])
        loads.append(
            pltpu.make_async_copy(p_hbm.at[span], p_ref.at[span], load_sem.at[4 + k])
        )
    for k in (0, 1, 4, 5, 6, 7, 2, 3):
        loads[k].start()

    def zero_if(absent, ref):
        @pl.when(absent)
        def _():
            ref[...] = jnp.zeros_like(ref)

    zero_if(gx == 0, rx_prev)
    zero_if(gx == 0, rc_prev)
    zero_if(gx == n_x - 1, rx_next)
    zero_if(gx == n_x - 1, rc_next)
    for side in (0, 1):
        dy = 2 * side - 1
        zero_if(jnp.logical_not(has[(0, dy)]), ry.at[side])
        for way in (0, 1):
            zero_if(jnp.logical_not(has[(2 * way - 1, dy)]), rd.at[side, way])

    moves = []

    def move(src, dst, dx, dy):
        slot = len(moves)
        target = {
            "gx": jnp.clip(gx + dx, 0, n_x - 1) if dx else gx,
            "gy": jnp.clip(gy + dy, 0, n_y - 1) if dy else gy,
        }
        copy = pltpu.make_async_remote_copy(
            src_ref=src, dst_ref=dst, send_sem=send_sem.at[slot], recv_sem=recv_sem.at[slot],
            device_id=target, device_id_type=MESH,
        )
        moves.append((copy, has[(dx, dy)], has[(-dx, -dy)]))

        @pl.when(has[(dx, dy)])
        def _():
            copy.start()

        return slot

    def arrive(slot):
        @pl.when(moves[slot][2])
        def _():
            moves[slot][0].wait_recv()

    loads[0].wait()
    loads[1].wait()
    x_top[half] = coef_ref[:, :HALO]
    x_bottom[half] = coef_ref[:, rows - HALO :]
    x_moves = []
    for k in range(CHUNKS):
        low, high = bounds[k + 1], bounds[k]
        loads[4 + k].wait()
        for m in range(low, min(high, half)):
            x_top[m] = p_ref[m, :, :HALO] * d_ref[:, :HALO]
            x_bottom[m] = p_ref[m, :, rows - HALO :] * d_ref[:, rows - HALO :]
        if k == 0:
            pl.semaphore_wait(barrier, group)
        span = pl.ds(low, high - low)
        x_moves.append(
            (
                move(x_top.at[span], rx_next.at[span], -1, 0),
                move(x_bottom.at[span], rx_prev.at[span], 1, 0),
                low, high,
            )
        )

    pick = lax.broadcasted_iota(jnp.int32, (cols, ccols), 0) // RATIO
    gather = jnp.where(
        pick == lax.broadcasted_iota(jnp.int32, (cols, ccols), 1), 1.0 / RATIO**2, 0.0
    ).astype(BF16)
    batch = next(k for k in (5, 3, 2, 1) if half % k == 0)

    def restrict(j, carry):
        tall = batch * levels * rows
        values = (p_ref[pl.ds(j * batch, batch)] * d_ref[...][None]).reshape(tall, cols)
        line[pl.ds(pl.multiple_of(j * tall, 8), tall)] = split_dot(values, gather)
        return carry

    lax.fori_loop(0, half // batch, restrict, 0)
    count = half * levels * crows
    coarse = line[pl.ds(0, count, stride=RATIO), :]
    for k in range(1, RATIO):
        coarse = coarse + line[pl.ds(k, count, stride=RATIO), :]
    loads[2].wait()
    wc[pl.ds(0, half)] = coarse.reshape(half, levels, crows, ccols)
    wc[half] = ccoef_ref[...]
    c_top[...] = wc[:, :, :HALO]
    c_bottom[...] = wc[:, :, crows - HALO :]
    c_moves = [move(c_top, rc_next, -1, 0), move(c_bottom, rc_prev, 1, 0)]

    flane = lax.broadcasted_iota(jnp.int32, (rows, LANES), 1)
    clane = lax.broadcasted_iota(jnp.int32, (crows, LANES), 1)
    fl = fr = jnp.zeros((rows, LANES), F32)
    cl = cr = jnp.zeros((crows, LANES), F32)
    for m in range(total):
        for level in range(levels):
            at = PASSES * (m * levels + level)
            if m < half:
                first = p_ref[m, level, :, :LANES] * d_ref[level, :, :LANES]
                last = p_ref[m, level, :, cols - LANES :] * d_ref[level, :, cols - LANES :]
            else:
                first = coef_ref[level, :, :LANES]
                last = coef_ref[level, :, cols - LANES :]
            fl = jnp.where(flane >= at, pltpu.roll(first, at, 1) if at else first, fl)
            fr = jnp.where(flane >= at, pltpu.roll(last, at + PASSES, 1), fr)
            field = wc[m, level]
            cl = jnp.where(
                clane >= at, pltpu.roll(field[:, :LANES], at, 1) if at else field[:, :LANES], cl
            )
            cr = jnp.where(clane >= at, pltpu.roll(field[:, ccols - LANES :], at + PASSES, 1), cr)
    for side, (fine, small) in enumerate(((fl, cl), (fr, cr))):
        strips[side, 0:crows] = small
        strips[side, crows : crows + rows] = fine
        strips[side, crows + rows :] = small
    y_moves = []
    for side in (0, 1):
        dy = 2 * side - 1
        other = 1 - side
        y_moves.append(move(strips.at[side, pl.ds(0, crows + rows)], ry.at[other], 0, dy))
        y_moves.append(move(strips.at[side, pl.ds(0, crows + 8)], rd.at[other, 1], -1, dy))
        y_moves.append(
            move(strips.at[side, pl.ds(crows + rows - 8, crows + 8)], rd.at[other, 0], 1, dy)
        )

    spread = jnp.where(
        lax.broadcasted_iota(jnp.int32, (ccols, cols), 1) // RATIO
        == lax.broadcasted_iota(jnp.int32, (ccols, cols), 0),
        1.0, 0.0,
    ).astype(BF16)
    acc[...] = jnp.zeros_like(acc)

    for slot in y_moves:
        arrive(slot)
    for slot in c_moves:
        arrive(slot)

    near = lax.broadcasted_iota(jnp.int32, (8, LANES), 0) < HALO
    for side in (0, 1):
        hyc[side, 0:crows] = ry[side, 0:crows]
        hyc[side, crows : crows + 8] = jnp.where(
            near, rd[side, 1, 0:8], rd[side, 0, crows : crows + 8]
        )
        hy[side, 0:rows] = ry[side, crows : crows + rows]
        hy[side, rows : rows + 8] = jnp.where(
            near, rd[side, 1, crows : crows + 8], rd[side, 0, 0:8]
        )

    def columns(ref, index, height):
        lane = lax.broadcasted_iota(jnp.int32, (height, LANES), 1)
        at = PASSES * index
        right = pltpu.roll(ref[1], LANES - at, 1)
        left = pltpu.roll(ref[0], LANES - PASSES - at, 1)
        return jnp.where(
            lane < PASSES, right, jnp.where(lane >= LANES - PASSES, left, 0.0)
        )

    def extended(main, nxt, prv, ref, index):
        height = main.shape[0] + 2 * HALO
        tall = jnp.concatenate([main, jnp.concatenate([nxt, prv], axis=0)], axis=0)
        return jnp.concatenate([tall, columns(ref, index, height)], axis=1)

    def coarse_field(m, level):
        return extended(
            wc[m, level], rc_next[m, level], rc_prev[m, level], hyc, m * levels + level
        )

    def fine_field(m, level, main):
        return extended(main, rx_next[m, level], rx_prev[m, level], hy, m * levels + level)

    ends = [
        value.astype(jnp.int32)
        for value in (has[(-1, 0)], has[(1, 0)], has[(0, -1)], has[(0, 1)])
    ]
    for k, value in enumerate(
        stencil_weights(coarse_field(half, 0), coarse_field(half, 1), crows, ccols, *ends)
    ):
        coarse_weights[k] = value

    def coarse_members(j, carry):
        for i in range(batch):
            m = j * batch + i
            for level in range(levels):
                u = apply_passes(coarse_field(m, level), [coarse_weights.at[k] for k in range(5)])
                line[pl.ds(pl.multiple_of((m * levels + level) * crows, 8), crows)] = u[
                    :crows, :ccols
                ]
        return carry

    lax.fori_loop(0, half // batch, coarse_members, 0)
    lanes_out[...] = split_dot(line[pl.ds(0, count)], spread)

    upper = lax.broadcasted_iota(jnp.int32, (2 * RATIO, cols), 0) < RATIO

    def fine_member(m, carry):
        for level in range(levels):
            u = apply_passes(
                fine_field(m, level, p_ref[m, level] * d_ref[level]),
                [fine_weights.at[k] for k in range(5)],
            )
            u = u[:rows, :cols]
            base = (m * levels + level) * crows
            for t in range(rows // (2 * RATIO)):
                a = jnp.broadcast_to(lanes_out[pl.ds(base + 2 * t, 1), :], (2 * RATIO, cols))
                b = jnp.broadcast_to(lanes_out[pl.ds(base + 2 * t + 1, 1), :], (2 * RATIO, cols))
                at = slice(2 * RATIO * t, 2 * RATIO * (t + 1))
                acc[level, at] += p_ref[m, level, at] * (u[at] + jnp.where(upper, a, b))
        return carry

    for k, (first, second, low, high) in enumerate(x_moves):
        arrive(first)
        arrive(second)
        if k == 0:
            for j, value in enumerate(
                stencil_weights(
                    fine_field(half, 0, coef_ref[0]), fine_field(half, 1, coef_ref[1]),
                    rows, cols, *ends
                )
            ):
                fine_weights[j] = value
        lax.fori_loop(low, min(high, half), fine_member, 0)

    swap = pltpu.make_async_remote_copy(
        src_ref=acc, dst_ref=acc_other, send_sem=send_sem.at[len(moves)],
        recv_sem=recv_sem.at[len(moves)], device_id={"ma": 1 - ma}, device_id_type=MESH,
    )
    swap.start()
    loads[3].wait()
    swap.wait_recv()
    d, r = d_ref[...], r_ref[...]
    q = d + (acc[...] + acc_other[...]) / (MEMBERS - 1)
    q_ref[...] = q

    def total_row(value):
        flat = value.reshape(levels * rows // 8, 8, cols)
        tile = jnp.sum(flat, axis=0)
        narrow = tile[:, :LANES]
        for k in range(1, cols // LANES):
            narrow = narrow + tile[:, k * LANES : (k + 1) * LANES]
        return jnp.sum(narrow, axis=0, keepdims=True)

    row = lax.broadcasted_iota(jnp.int32, (8, LANES), 0)
    packed = jnp.zeros((8, LANES), F32)
    for k, value in enumerate((r * r, d * q, r * q, q * q)):
        packed = jnp.where(row == k, total_row(value), packed)
    part[...] = packed
    slots[me] = packed

    def to_peer(k):
        return pltpu.make_async_remote_copy(
            src_ref=part, dst_ref=slots.at[me], send_sem=group_send.at[k],
            recv_sem=group_recv.at[me],
            device_id={"gx": k // n_y, "gy": k % n_y}, device_id_type=MESH,
        )

    def from_peer(k):
        return pltpu.make_async_remote_copy(
            src_ref=part, dst_ref=slots.at[k], send_sem=group_send.at[k],
            recv_sem=group_recv.at[k],
            device_id={"gx": k // n_y, "gy": k % n_y}, device_id_type=MESH,
        )

    each_peer(lambda k: to_peer(k).start())
    swap.wait_send()
    for copy, sends, _ in moves:
        @pl.when(sends)
        def _():
            copy.wait_send()
    each_peer(lambda k: from_peer(k).wait_recv())
    sums = jnp.sum(jnp.sum(slots[...], axis=0), axis=1, keepdims=True)
    norm_old, curvature, cross, image = (sums[k : k + 1] for k in range(4))
    step_length = norm_old / curvature
    norm_new = norm_old + step_length * (step_length * image - 2.0 * cross)
    step_ref[...] = jnp.broadcast_to(step_length, (1, cols))
    growth_ref[...] = jnp.broadcast_to(norm_new / norm_old, (1, cols))
    each_peer(lambda k: to_peer(k).wait_send())


def local(n_x, n_y, perturbations, coefficients, coarse_coefficients, iterate, residual, direction):
    half, levels, rows, cols = perturbations.shape
    _, crows, ccols = coarse_coefficients.shape
    total = half + 1
    group = n_x * n_y
    n_moves = 2 * CHUNKS + 2 + 6 + 1
    vmem = pl.BlockSpec(memory_space=pltpu.VMEM)
    q, step_length, growth = pl.pallas_call(
        functools.partial(kernel, (n_x, n_y)),
        out_shape=(
            jax.ShapeDtypeStruct((levels, rows, cols), F32),
            jax.ShapeDtypeStruct((1, cols), F32),
            jax.ShapeDtypeStruct((1, cols), F32),
        ),
        in_specs=[pl.BlockSpec(memory_space=pltpu.HBM)] * 5,
        out_specs=(vmem, vmem, vmem),
        scratch_shapes=[
            pltpu.VMEM((half, levels, rows, cols), F32),
            pltpu.VMEM((2, rows, cols), F32),
            pltpu.VMEM((2, crows, ccols), F32),
            pltpu.VMEM((levels, rows, cols), F32),
            pltpu.VMEM((levels, rows, cols), F32),
            pltpu.VMEM((total, levels, crows, ccols), F32),
            pltpu.VMEM((half * levels * rows, ccols), F32),
            pltpu.VMEM((half * levels * crows, cols), F32),
            pltpu.VMEM((total, levels, HALO, cols), F32),
            pltpu.VMEM((total, levels, HALO, cols), F32),
            pltpu.VMEM((total, levels, HALO, ccols), F32),
            pltpu.VMEM((total, levels, HALO, ccols), F32),
            pltpu.VMEM((2, rows + 2 * crows, LANES), F32),
            pltpu.VMEM((total, levels, HALO, cols), F32),
            pltpu.VMEM((total, levels, HALO, cols), F32),
            pltpu.VMEM((total, levels, HALO, ccols), F32),
            pltpu.VMEM((total, levels, HALO, ccols), F32),
            pltpu.VMEM((2, rows + crows, LANES), F32),
            pltpu.VMEM((2, 2, crows + 8, LANES), F32),
            pltpu.VMEM((2, rows + 2 * HALO, LANES), F32),
            pltpu.VMEM((2, crows + 2 * HALO, LANES), F32),
            pltpu.VMEM((5, rows + 2 * HALO, cols + LANES), F32),
            pltpu.VMEM((5, crows + 2 * HALO, ccols + LANES), F32),
            pltpu.VMEM((levels, rows, cols), F32),
            pltpu.VMEM((levels, rows, cols), F32),
            pltpu.VMEM((8, LANES), F32),
            pltpu.VMEM((group, 8, LANES), F32),
            pltpu.SemaphoreType.DMA((4 + CHUNKS,)),
            pltpu.SemaphoreType.DMA((n_moves,)),
            pltpu.SemaphoreType.DMA((n_moves,)),
            pltpu.SemaphoreType.DMA((group,)),
            pltpu.SemaphoreType.DMA((group,)),
        ],
        compiler_params=pltpu.CompilerParams(
            collective_id=0, has_side_effects=True, vmem_limit_bytes=62 << 20
        ),
    )(perturbations, coefficients, coarse_coefficients, residual, direction)
    new_iterate = iterate + step_length * direction
    new_residual = residual - step_length * q
    new_direction = new_residual + growth * direction
    return (new_iterate, new_residual, new_direction)


def solution(mesh):
    cell = P(None, "gx", "gy")
    return jax.shard_map(
        functools.partial(local, mesh.shape["gx"], mesh.shape["gy"]),
        mesh=mesh,
        in_specs=(P("ma", None, "gx", "gy"), cell, cell, cell, cell, cell),
        out_specs=(cell, cell, cell),
        check_vma=False,
    )
```

```python
import functools

import jax
import jax.numpy as jnp
from jax import lax
from jax.experimental import pallas as pl
from jax.experimental.pallas import tpu as pltpu
from jax.sharding import PartitionSpec as P

MEMBERS = 30
PASSES = 3
RATIO = 4
HALO = 4
LANES = 128
CHUNKS = 4
MESH = pl.DeviceIdType.MESH
F32 = jnp.float32
BF16 = jnp.bfloat16


def shift_up(u, axis):
    return pltpu.roll(u, u.shape[axis] - 1, axis)


def shift_down(u, axis):
    return pltpu.roll(u, 1, axis)


def split_dot(a, b):
    high = a.astype(BF16)
    low = (a - high.astype(F32)).astype(BF16)
    return jnp.dot(high, b, preferred_element_type=F32) + jnp.dot(
        low, b, preferred_element_type=F32
    )


def stencil_weights(cx, cy, rows, cols, has_prev, has_next, has_left, has_right):
    ext_rows, ext_cols = cx.shape
    row = lax.broadcasted_iota(jnp.int32, (ext_rows, ext_cols), 0)
    col = lax.broadcasted_iota(jnp.int32, (ext_rows, ext_cols), 1)
    outside = (
        ((row >= rows) & (row < rows + HALO) & (has_next == 0))
        | ((row >= rows + HALO) & (has_prev == 0))
        | ((col >= cols) & (col < cols + LANES // 2) & (has_right == 0))
        | ((col >= cols + LANES // 2) & (has_left == 0))
    )
    xp = 0.5 * (cx + shift_up(cx, 0))
    xm = shift_down(xp, 0)
    yp = 0.5 * (cy + shift_up(cy, 1))
    ym = shift_down(yp, 1)
    centre = 1.0 - xp - xm - yp - ym
    return [jnp.where(outside, 0.0, value) for value in (centre, xp, xm, yp, ym)]


def apply_passes(u, weights):
    for _ in range(PASSES):
        u = (
            weights[0][...] * u
            + weights[1][...] * shift_up(u, 0)
            + weights[2][...] * shift_down(u, 0)
            + weights[3][...] * shift_up(u, 1)
            + weights[4][...] * shift_down(u, 1)
        )
    return u


def kernel(
    sizes,
    p_hbm, coef_hbm, ccoef_hbm, r_hbm, d_hbm,
    q_ref, step_ref, growth_ref,
    p_ref, coef_ref, ccoef_ref, r_ref, d_ref,
    wc, line, lanes_out,
    x_top, x_bottom, c_top, c_bottom, strips,
    rx_next, rx_prev, rc_next, rc_prev, ry, rd,
    hy, hyc, fine_weights, coarse_weights,
    acc, acc_other, part, slots,
    load_sem, send_sem, recv_sem, group_send, group_recv,
):
    n_x, n_y = sizes
    half, levels, rows, cols = p_ref.shape
    crows, ccols = ccoef_ref.shape[1], ccoef_ref.shape[2]
    gx, gy, ma = lax.axis_index("gx"), lax.axis_index("gy"), lax.axis_index("ma")
    me = gx * n_y + gy
    group = n_x * n_y
    has = {
        (-1, 0): gx > 0, (1, 0): gx < n_x - 1, (0, -1): gy > 0, (0, 1): gy < n_y - 1,
    }
    for dx in (-1, 1):
        for dy in (-1, 1):
            has[(dx, dy)] = has[(dx, 0)] & has[(0, dy)]

    def each_peer(action):
        def body(step, carry):
            action(lax.rem(me + step, group))
            return carry

        lax.fori_loop(1, group, body, 0, unroll=group <= 16)

    total = half + 1
    bounds = [total - (total * k) // CHUNKS for k in range(CHUNKS + 1)]
    loads = [
        pltpu.make_async_copy(src, dst, load_sem.at[k])
        for k, (src, dst) in enumerate(
            ((d_hbm, d_ref), (coef_hbm, coef_ref), (ccoef_hbm, ccoef_ref), (r_hbm, r_ref))
        )
    ]
    for k in range(CHUNKS):
        span = pl.ds(bounds[k + 1], min(bounds[k], half) - bounds[k + 1])
        loads.append(
            pltpu.make_async_copy(p_hbm.at[span], p_ref.at[span], load_sem.at[4 + k])
        )
    for k in (0, 1, 4, 5, 6, 7, 2, 3):
        loads[k].start()

    barrier = pltpu.get_barrier_semaphore()
    pl.semaphore_signal(barrier, inc=1, device_id={"ma": 1 - ma}, device_id_type=MESH)
    each_peer(
        lambda k: pl.semaphore_signal(
            barrier, inc=1, device_id={"gx": k // n_y, "gy": k % n_y}, device_id_type=MESH
        )
    )

    def zero_if(absent, ref):
        @pl.when(absent)
        def _():
            ref[...] = jnp.zeros_like(ref)

    zero_if(gx == 0, rx_prev)
    zero_if(gx == 0, rc_prev)
    zero_if(gx == n_x - 1, rx_next)
    zero_if(gx == n_x - 1, rc_next)
    for side in (0, 1):
        dy = 2 * side - 1
        zero_if(jnp.logical_not(has[(0, dy)]), ry.at[side])
        for way in (0, 1):
            zero_if(jnp.logical_not(has[(2 * way - 1, dy)]), rd.at[side, way])

    moves = []

    def move(src, dst, dx, dy):
        slot = len(moves)
        target = {
            "gx": jnp.clip(gx + dx, 0, n_x - 1) if dx else gx,
            "gy": jnp.clip(gy + dy, 0, n_y - 1) if dy else gy,
        }
        copy = pltpu.make_async_remote_copy(
            src_ref=src, dst_ref=dst, send_sem=send_sem.at[slot], recv_sem=recv_sem.at[slot],
            device_id=target, device_id_type=MESH,
        )
        moves.append((copy, has[(dx, dy)], has[(-dx, -dy)]))

        @pl.when(has[(dx, dy)])
        def _():
            copy.start()

        return slot

    def arrive(slot):
        @pl.when(moves[slot][2])
        def _():
            moves[slot][0].wait_recv()

    loads[0].wait()
    loads[1].wait()
    x_top[half] = coef_ref[:, :HALO]
    x_bottom[half] = coef_ref[:, rows - HALO :]
    for k in range(CHUNKS):
        low, high = bounds[k + 1], bounds[k]
        loads[4 + k].wait()
        for m in range(low, min(high, half)):
            x_top[m] = p_ref[m, :, :HALO] * d_ref[:, :HALO]
            x_bottom[m] = p_ref[m, :, rows - HALO :] * d_ref[:, rows - HALO :]

    pick = lax.broadcasted_iota(jnp.int32, (cols, ccols), 0) // RATIO
    gather = jnp.where(
        pick == lax.broadcasted_iota(jnp.int32, (cols, ccols), 1), 1.0 / RATIO**2, 0.0
    ).astype(BF16)
    batch = next(k for k in (5, 3, 2, 1) if half % k == 0)

    def restrict(j, carry):
        tall = batch * levels * rows
        values = (p_ref[pl.ds(j * batch, batch)] * d_ref[...][None]).reshape(tall, cols)
        line[pl.ds(pl.multiple_of(j * tall, 8), tall)] = split_dot(values, gather)
        return carry

    lax.fori_loop(0, half // batch, restrict, 0)
    count = half * levels * crows
    coarse = line[pl.ds(0, count, stride=RATIO), :]
    for k in range(1, RATIO):
        coarse = coarse + line[pl.ds(k, count, stride=RATIO), :]
    loads[2].wait()
    wc[pl.ds(0, half)] = coarse.reshape(half, levels, crows, ccols)
    wc[half] = ccoef_ref[...]
    c_top[...] = wc[:, :, :HALO]
    c_bottom[...] = wc[:, :, crows - HALO :]

    flane = lax.broadcasted_iota(jnp.int32, (rows, LANES), 1)
    clane = lax.broadcasted_iota(jnp.int32, (crows, LANES), 1)
    fl = fr = jnp.zeros((rows, LANES), F32)
    cl = cr = jnp.zeros((crows, LANES), F32)
    for m in range(total):
        for level in range(levels):
            at = PASSES * (m * levels + level)
            if m < half:
                first = p_ref[m, level, :, :LANES] * d_ref[level, :, :LANES]
                last = p_ref[m, level, :, cols - LANES :] * d_ref[level, :, cols - LANES :]
            else:
                first = coef_ref[level, :, :LANES]
                last = coef_ref[level, :, cols - LANES :]
            fl = jnp.where(flane >= at, pltpu.roll(first, at, 1) if at else first, fl)
            fr = jnp.where(flane >= at, pltpu.roll(last, at + PASSES, 1), fr)
            field = wc[m, level]
            cl = jnp.where(
                clane >= at, pltpu.roll(field[:, :LANES], at, 1) if at else field[:, :LANES], cl
            )
            cr = jnp.where(clane >= at, pltpu.roll(field[:, ccols - LANES :], at + PASSES, 1), cr)
    for side, (fine, small) in enumerate(((fl, cl), (fr, cr))):
        strips[side, 0:crows] = small
        strips[side, crows : crows + rows] = fine
        strips[side, crows + rows :] = small
    pl.semaphore_wait(barrier, group)
    y_moves = []
    for side in (0, 1):
        dy = 2 * side - 1
        other = 1 - side
        y_moves.append(move(strips.at[side, pl.ds(0, crows + rows)], ry.at[other], 0, dy))
        y_moves.append(move(strips.at[side, pl.ds(0, crows + 8)], rd.at[other, 1], -1, dy))
        y_moves.append(
            move(strips.at[side, pl.ds(crows + rows - 8, crows + 8)], rd.at[other, 0], 1, dy)
        )

    c_moves = [move(c_top, rc_next, -1, 0), move(c_bottom, rc_prev, 1, 0)]
    x_moves = []
    for k in range(CHUNKS):
        low, high = bounds[k + 1], bounds[k]
        span = pl.ds(low, high - low)
        x_moves.append(
            (
                move(x_top.at[span], rx_next.at[span], -1, 0),
                move(x_bottom.at[span], rx_prev.at[span], 1, 0),
                low, high,
            )
        )

    spread = jnp.where(
        lax.broadcasted_iota(jnp.int32, (ccols, cols), 1) // RATIO
        == lax.broadcasted_iota(jnp.int32, (ccols, cols), 0),
        1.0, 0.0,
    ).astype(BF16)
    acc[...] = jnp.zeros_like(acc)

    for slot in y_moves:
        arrive(slot)
    for slot in c_moves:
        arrive(slot)

    near = lax.broadcasted_iota(jnp.int32, (8, LANES), 0) < HALO
    for side in (0, 1):
        hyc[side, 0:crows] = ry[side, 0:crows]
        hyc[side, crows : crows + 8] = jnp.where(
            near, rd[side, 1, 0:8], rd[side, 0, crows : crows + 8]
        )
        hy[side, 0:rows] = ry[side, crows : crows + rows]
        hy[side, rows : rows + 8] = jnp.where(
            near, rd[side, 1, crows : crows + 8], rd[side, 0, 0:8]
        )

    def columns(ref, index, height):
        lane = lax.broadcasted_iota(jnp.int32, (height, LANES), 1)
        at = PASSES * index
        right = pltpu.roll(ref[1], LANES - at, 1)
        left = pltpu.roll(ref[0], LANES - PASSES - at, 1)
        return jnp.where(
            lane < PASSES, right, jnp.where(lane >= LANES - PASSES, left, 0.0)
        )

    def extended(main, nxt, prv, ref, index):
        height = main.shape[0] + 2 * HALO
        tall = jnp.concatenate([main, jnp.concatenate([nxt, prv], axis=0)], axis=0)
        return jnp.concatenate([tall, columns(ref, index, height)], axis=1)

    def coarse_field(m, level):
        return extended(
            wc[m, level], rc_next[m, level], rc_prev[m, level], hyc, m * levels + level
        )

    def fine_field(m, level, main):
        return extended(main, rx_next[m, level], rx_prev[m, level], hy, m * levels + level)

    ends = [
        value.astype(jnp.int32)
        for value in (has[(-1, 0)], has[(1, 0)], has[(0, -1)], has[(0, 1)])
    ]
    for k, value in enumerate(
        stencil_weights(coarse_field(half, 0), coarse_field(half, 1), crows, ccols, *ends)
    ):
        coarse_weights[k] = value

    def coarse_members(j, carry):
        for i in range(batch):
            m = j * batch + i
            for level in range(levels):
                u = apply_passes(coarse_field(m, level), [coarse_weights.at[k] for k in range(5)])
                line[pl.ds(pl.multiple_of((m * levels + level) * crows, 8), crows)] = u[
                    :crows, :ccols
                ]
        return carry

    lax.fori_loop(0, half // batch, coarse_members, 0)
    lanes_out[...] = split_dot(line[pl.ds(0, count)], spread)

    upper = lax.broadcasted_iota(jnp.int32, (2 * RATIO, cols), 0) < RATIO

    def fine_member(m, carry):
        for level in range(levels):
            u = apply_passes(
                fine_field(m, level, p_ref[m, level] * d_ref[level]),
                [fine_weights.at[k] for k in range(5)],
            )
            u = u[:rows, :cols]
            base = (m * levels + level) * crows
            for t in range(rows // (2 * RATIO)):
                a = jnp.broadcast_to(lanes_out[pl.ds(base + 2 * t, 1), :], (2 * RATIO, cols))
                b = jnp.broadcast_to(lanes_out[pl.ds(base + 2 * t + 1, 1), :], (2 * RATIO, cols))
                at = slice(2 * RATIO * t, 2 * RATIO * (t + 1))
                acc[level, at] += p_ref[m, level, at] * (u[at] + jnp.where(upper, a, b))
        return carry

    for k, (first, second, low, high) in enumerate(x_moves):
        arrive(first)
        arrive(second)
        if k == 0:
            for j, value in enumerate(
                stencil_weights(
                    fine_field(half, 0, coef_ref[0]), fine_field(half, 1, coef_ref[1]),
                    rows, cols, *ends
                )
            ):
                fine_weights[j] = value
        lax.fori_loop(low, min(high, half), fine_member, 0)

    swap = pltpu.make_async_remote_copy(
        src_ref=acc, dst_ref=acc_other, send_sem=send_sem.at[len(moves)],
        recv_sem=recv_sem.at[len(moves)], device_id={"ma": 1 - ma}, device_id_type=MESH,
    )
    swap.start()
    loads[3].wait()
    swap.wait_recv()
    d, r = d_ref[...], r_ref[...]
    q = d + (acc[...] + acc_other[...]) / (MEMBERS - 1)
    q_ref[...] = q

    def total_row(value):
        flat = value.reshape(levels * rows // 8, 8, cols)
        tile = jnp.sum(flat, axis=0)
        narrow = tile[:, :LANES]
        for k in range(1, cols // LANES):
            narrow = narrow + tile[:, k * LANES : (k + 1) * LANES]
        return jnp.sum(narrow, axis=0, keepdims=True)

    row = lax.broadcasted_iota(jnp.int32, (8, LANES), 0)
    packed = jnp.zeros((8, LANES), F32)
    for k, value in enumerate((r * r, d * q, r * q, q * q)):
        packed = jnp.where(row == k, total_row(value), packed)
    part[...] = packed
    slots[me] = packed

    def to_peer(k):
        return pltpu.make_async_remote_copy(
            src_ref=part, dst_ref=slots.at[me], send_sem=group_send.at[k],
            recv_sem=group_recv.at[me],
            device_id={"gx": k // n_y, "gy": k % n_y}, device_id_type=MESH,
        )

    def from_peer(k):
        return pltpu.make_async_remote_copy(
            src_ref=part, dst_ref=slots.at[k], send_sem=group_send.at[k],
            recv_sem=group_recv.at[k],
            device_id={"gx": k // n_y, "gy": k % n_y}, device_id_type=MESH,
        )

    each_peer(lambda k: to_peer(k).start())
    swap.wait_send()
    for copy, sends, _ in moves:
        @pl.when(sends)
        def _():
            copy.wait_send()
    each_peer(lambda k: from_peer(k).wait_recv())
    sums = jnp.sum(jnp.sum(slots[...], axis=0), axis=1, keepdims=True)
    norm_old, curvature, cross, image = (sums[k : k + 1] for k in range(4))
    step_length = norm_old / curvature
    norm_new = norm_old + step_length * (step_length * image - 2.0 * cross)
    step_ref[...] = jnp.broadcast_to(step_length, (1, cols))
    growth_ref[...] = jnp.broadcast_to(norm_new / norm_old, (1, cols))
    each_peer(lambda k: to_peer(k).wait_send())


def local(n_x, n_y, perturbations, coefficients, coarse_coefficients, iterate, residual, direction):
    half, levels, rows, cols = perturbations.shape
    _, crows, ccols = coarse_coefficients.shape
    total = half + 1
    group = n_x * n_y
    n_moves = 2 * CHUNKS + 2 + 6 + 1
    vmem = pl.BlockSpec(memory_space=pltpu.VMEM)
    q, step_length, growth = pl.pallas_call(
        functools.partial(kernel, (n_x, n_y)),
        out_shape=(
            jax.ShapeDtypeStruct((levels, rows, cols), F32),
            jax.ShapeDtypeStruct((1, cols), F32),
            jax.ShapeDtypeStruct((1, cols), F32),
        ),
        in_specs=[pl.BlockSpec(memory_space=pltpu.HBM)] * 5,
        out_specs=(vmem, vmem, vmem),
        scratch_shapes=[
            pltpu.VMEM((half, levels, rows, cols), F32),
            pltpu.VMEM((2, rows, cols), F32),
            pltpu.VMEM((2, crows, ccols), F32),
            pltpu.VMEM((levels, rows, cols), F32),
            pltpu.VMEM((levels, rows, cols), F32),
            pltpu.VMEM((total, levels, crows, ccols), F32),
            pltpu.VMEM((half * levels * rows, ccols), F32),
            pltpu.VMEM((half * levels * crows, cols), F32),
            pltpu.VMEM((total, levels, HALO, cols), F32),
            pltpu.VMEM((total, levels, HALO, cols), F32),
            pltpu.VMEM((total, levels, HALO, ccols), F32),
            pltpu.VMEM((total, levels, HALO, ccols), F32),
            pltpu.VMEM((2, rows + 2 * crows, LANES), F32),
            pltpu.VMEM((total, levels, HALO, cols), F32),
            pltpu.VMEM((total, levels, HALO, cols), F32),
            pltpu.VMEM((total, levels, HALO, ccols), F32),
            pltpu.VMEM((total, levels, HALO, ccols), F32),
            pltpu.VMEM((2, rows + crows, LANES), F32),
            pltpu.VMEM((2, 2, crows + 8, LANES), F32),
            pltpu.VMEM((2, rows + 2 * HALO, LANES), F32),
            pltpu.VMEM((2, crows + 2 * HALO, LANES), F32),
            pltpu.VMEM((5, rows + 2 * HALO, cols + LANES), F32),
            pltpu.VMEM((5, crows + 2 * HALO, ccols + LANES), F32),
            pltpu.VMEM((levels, rows, cols), F32),
            pltpu.VMEM((levels, rows, cols), F32),
            pltpu.VMEM((8, LANES), F32),
            pltpu.VMEM((group, 8, LANES), F32),
            pltpu.SemaphoreType.DMA((4 + CHUNKS,)),
            pltpu.SemaphoreType.DMA((n_moves,)),
            pltpu.SemaphoreType.DMA((n_moves,)),
            pltpu.SemaphoreType.DMA((group,)),
            pltpu.SemaphoreType.DMA((group,)),
        ],
        compiler_params=pltpu.CompilerParams(
            collective_id=0, has_side_effects=True, vmem_limit_bytes=62 << 20
        ),
    )(perturbations, coefficients, coarse_coefficients, residual, direction)
    new_iterate = iterate + step_length * direction
    new_residual = residual - step_length * q
    new_direction = new_residual + growth * direction
    return (new_iterate, new_residual, new_direction)


def solution(mesh):
    cell = P(None, "gx", "gy")
    return jax.shard_map(
        functools.partial(local, mesh.shape["gx"], mesh.shape["gy"]),
        mesh=mesh,
        in_specs=(P("ma", None, "gx", "gy"), cell, cell, cell, cell, cell),
        out_specs=(cell, cell, cell),
        check_vma=False,
    )
```

```python
import functools

import jax
import jax.numpy as jnp
from jax import lax
from jax.experimental import pallas as pl
from jax.experimental.pallas import tpu as pltpu
from jax.sharding import PartitionSpec as P

MEMBERS = 30
PASSES = 3
RATIO = 4
HALO = 4
LANES = 128
CHUNKS = 4
MESH = pl.DeviceIdType.MESH
F32 = jnp.float32
BF16 = jnp.bfloat16


def shift_up(u, axis):
    return pltpu.roll(u, u.shape[axis] - 1, axis)


def shift_down(u, axis):
    return pltpu.roll(u, 1, axis)


def split_dot(a, b):
    high = a.astype(BF16)
    low = (a - high.astype(F32)).astype(BF16)
    return jnp.dot(high, b, preferred_element_type=F32) + jnp.dot(
        low, b, preferred_element_type=F32
    )


def stencil_weights(cx, cy, rows, cols, has_prev, has_next, has_left, has_right):
    ext_rows, ext_cols = cx.shape
    row = lax.broadcasted_iota(jnp.int32, (ext_rows, ext_cols), 0)
    col = lax.broadcasted_iota(jnp.int32, (ext_rows, ext_cols), 1)
    outside = (
        ((row >= rows) & (row < rows + HALO) & (has_next == 0))
        | ((row >= rows + HALO) & (has_prev == 0))
        | ((col >= cols) & (col < cols + LANES // 2) & (has_right == 0))
        | ((col >= cols + LANES // 2) & (has_left == 0))
    )
    xp = 0.5 * (cx + shift_up(cx, 0))
    xm = shift_down(xp, 0)
    yp = 0.5 * (cy + shift_up(cy, 1))
    ym = shift_down(yp, 1)
    centre = 1.0 - xp - xm - yp - ym
    return [jnp.where(outside, 0.0, value) for value in (centre, xp, xm, yp, ym)]


def apply_passes(u, weights):
    for _ in range(PASSES):
        u = (
            weights[0][...] * u
            + weights[1][...] * shift_up(u, 0)
            + weights[2][...] * shift_down(u, 0)
            + weights[3][...] * shift_up(u, 1)
            + weights[4][...] * shift_down(u, 1)
        )
    return u


def kernel(
    sizes,
    p_hbm, coef_hbm, ccoef_hbm, r_hbm, d_hbm,
    q_ref, step_ref, growth_ref,
    p_ref, coef_ref, ccoef_ref, r_ref, d_ref,
    wc, line, lanes_out,
    x_top, x_bottom, c_top, c_bottom, strips,
    rx_next, rx_prev, rc_next, rc_prev, ry, rd,
    hy, hyc, fine_weights, coarse_weights,
    acc, acc_other, part, slots,
    load_sem, send_sem, recv_sem, group_send, group_recv,
):
    n_x, n_y = sizes
    half, levels, rows, cols = p_ref.shape
    crows, ccols = ccoef_ref.shape[1], ccoef_ref.shape[2]
    gx, gy, ma = lax.axis_index("gx"), lax.axis_index("gy"), lax.axis_index("ma")
    me = gx * n_y + gy
    group = n_x * n_y
    has = {
        (-1, 0): gx > 0, (1, 0): gx < n_x - 1, (0, -1): gy > 0, (0, 1): gy < n_y - 1,
    }
    for dx in (-1, 1):
        for dy in (-1, 1):
            has[(dx, dy)] = has[(dx, 0)] & has[(0, dy)]

    def each_peer(action):
        def body(step, carry):
            action(lax.rem(me + step, group))
            return carry

        lax.fori_loop(1, group, body, 0, unroll=group <= 16)

    total = half + 1
    bounds = [total - (total * k) // CHUNKS for k in range(CHUNKS + 1)]
    loads = [
        pltpu.make_async_copy(src, dst, load_sem.at[k])
        for k, (src, dst) in enumerate(
            ((d_hbm, d_ref), (coef_hbm, coef_ref), (ccoef_hbm, ccoef_ref), (r_hbm, r_ref))
        )
    ]
    for k in range(CHUNKS):
        span = pl.ds(bounds[k + 1], min(bounds[k], half) - bounds[k + 1])
        loads.append(
            pltpu.make_async_copy(p_hbm.at[span], p_ref.at[span], load_sem.at[4 + k])
        )
    for k in (0, 1, 4, 5, 6, 7, 2, 3):
        loads[k].start()

    barrier = pltpu.get_barrier_semaphore()
    pl.semaphore_signal(barrier, inc=1, device_id={"ma": 1 - ma}, device_id_type=MESH)
    each_peer(
        lambda k: pl.semaphore_signal(
            barrier, inc=1, device_id={"gx": k // n_y, "gy": k % n_y}, device_id_type=MESH
        )
    )

    def zero_if(absent, ref):
        @pl.when(absent)
        def _():
            ref[...] = jnp.zeros_like(ref)

    zero_if(gx == 0, rx_prev)
    zero_if(gx == 0, rc_prev)
    zero_if(gx == n_x - 1, rx_next)
    zero_if(gx == n_x - 1, rc_next)
    for side in (0, 1):
        dy = 2 * side - 1
        zero_if(jnp.logical_not(has[(0, dy)]), ry.at[side])
        for way in (0, 1):
            zero_if(jnp.logical_not(has[(2 * way - 1, dy)]), rd.at[side, way])

    moves = []

    def move(src, dst, dx, dy):
        slot = len(moves)
        target = {
            "gx": jnp.clip(gx + dx, 0, n_x - 1) if dx else gx,
            "gy": jnp.clip(gy + dy, 0, n_y - 1) if dy else gy,
        }
        copy = pltpu.make_async_remote_copy(
            src_ref=src, dst_ref=dst, send_sem=send_sem.at[slot], recv_sem=recv_sem.at[slot],
            device_id=target, device_id_type=MESH,
        )
        moves.append((copy, has[(dx, dy)], has[(-dx, -dy)]))

        @pl.when(has[(dx, dy)])
        def _():
            copy.start()

        return slot

    def arrive(slot):
        @pl.when(moves[slot][2])
        def _():
            moves[slot][0].wait_recv()

    loads[0].wait()
    loads[1].wait()
    x_top[half] = coef_ref[:, :HALO]
    x_bottom[half] = coef_ref[:, rows - HALO :]
    for k in range(CHUNKS):
        low, high = bounds[k + 1], bounds[k]
        loads[4 + k].wait()
        for m in range(low, min(high, half)):
            x_top[m] = p_ref[m, :, :HALO] * d_ref[:, :HALO]
            x_bottom[m] = p_ref[m, :, rows - HALO :] * d_ref[:, rows - HALO :]

    pick = lax.broadcasted_iota(jnp.int32, (cols, ccols), 0) // RATIO
    gather = jnp.where(
        pick == lax.broadcasted_iota(jnp.int32, (cols, ccols), 1), 1.0 / RATIO**2, 0.0
    ).astype(BF16)
    batch = next(k for k in (5, 3, 2, 1) if half % k == 0)

    def restrict(j, carry):
        tall = batch * levels * rows
        values = (p_ref[pl.ds(j * batch, batch)] * d_ref[...][None]).reshape(tall, cols)
        line[pl.ds(pl.multiple_of(j * tall, 8), tall)] = split_dot(values, gather)
        return carry

    lax.fori_loop(0, half // batch, restrict, 0)
    count = half * levels * crows
    coarse = line[pl.ds(0, count, stride=RATIO), :]
    for k in range(1, RATIO):
        coarse = coarse + line[pl.ds(k, count, stride=RATIO), :]
    loads[2].wait()
    wc[pl.ds(0, half)] = coarse.reshape(half, levels, crows, ccols)
    wc[half] = ccoef_ref[...]
    c_top[...] = wc[:, :, :HALO]
    c_bottom[...] = wc[:, :, crows - HALO :]

    flane = lax.broadcasted_iota(jnp.int32, (rows, LANES), 1)
    clane = lax.broadcasted_iota(jnp.int32, (crows, LANES), 1)
    fl = fr = jnp.zeros((rows, LANES), F32)
    cl = cr = jnp.zeros((crows, LANES), F32)
    for m in range(total):
        for level in range(levels):
            at = PASSES * (m * levels + level)
            if m < half:
                first = p_ref[m, level, :, :LANES] * d_ref[level, :, :LANES]
                last = p_ref[m, level, :, cols - LANES :] * d_ref[level, :, cols - LANES :]
            else:
                first = coef_ref[level, :, :LANES]
                last = coef_ref[level, :, cols - LANES :]
            fl = jnp.where(flane >= at, pltpu.roll(first, at, 1) if at else first, fl)
            fr = jnp.where(flane >= at, pltpu.roll(last, at + PASSES, 1), fr)
            field = wc[m, level]
            cl = jnp.where(
                clane >= at, pltpu.roll(field[:, :LANES], at, 1) if at else field[:, :LANES], cl
            )
            cr = jnp.where(clane >= at, pltpu.roll(field[:, ccols - LANES :], at + PASSES, 1), cr)
    for side, (fine, small) in enumerate(((fl, cl), (fr, cr))):
        strips[side, 0:crows] = small
        strips[side, crows : crows + rows] = fine
        strips[side, crows + rows :] = small
    pl.semaphore_wait(barrier, group)
    y_moves = []
    for side in (0, 1):
        dy = 2 * side - 1
        other = 1 - side
        y_moves.append(move(strips.at[side, pl.ds(0, crows + rows)], ry.at[other], 0, dy))
        y_moves.append(move(strips.at[side, pl.ds(0, crows + 8)], rd.at[other, 1], -1, dy))
        y_moves.append(
            move(strips.at[side, pl.ds(crows + rows - 8, crows + 8)], rd.at[other, 0], 1, dy)
        )

    c_moves = [move(c_top, rc_next, -1, 0), move(c_bottom, rc_prev, 1, 0)]
    x_moves = []
    for k in range(CHUNKS):
        low, high = bounds[k + 1], bounds[k]
        span = pl.ds(low, high - low)
        x_moves.append(
            (
                move(x_top.at[span], rx_next.at[span], -1, 0),
                move(x_bottom.at[span], rx_prev.at[span], 1, 0),
                low, high,
            )
        )

    spread = jnp.where(
        lax.broadcasted_iota(jnp.int32, (ccols, cols), 1) // RATIO
        == lax.broadcasted_iota(jnp.int32, (ccols, cols), 0),
        1.0, 0.0,
    ).astype(BF16)
    acc[...] = jnp.zeros_like(acc)

    for slot in y_moves:
        arrive(slot)
    for slot in c_moves:
        arrive(slot)

    near = lax.broadcasted_iota(jnp.int32, (8, LANES), 0) < HALO
    for side in (0, 1):
        hyc[side, 0:crows] = ry[side, 0:crows]
        hyc[side, crows : crows + 8] = jnp.where(
            near, rd[side, 1, 0:8], rd[side, 0, crows : crows + 8]
        )
        hy[side, 0:rows] = ry[side, crows : crows + rows]
        hy[side, rows : rows + 8] = jnp.where(
            near, rd[side, 1, crows : crows + 8], rd[side, 0, 0:8]
        )

    def columns(ref, index, height):
        lane = lax.broadcasted_iota(jnp.int32, (height, LANES), 1)
        at = PASSES * index
        right = pltpu.roll(ref[1], LANES - at, 1)
        left = pltpu.roll(ref[0], LANES - PASSES - at, 1)
        return jnp.where(
            lane < PASSES, right, jnp.where(lane >= LANES - PASSES, left, 0.0)
        )

    def extended(main, nxt, prv, ref, index):
        height = main.shape[0] + 2 * HALO
        tall = jnp.concatenate([main, jnp.concatenate([nxt, prv], axis=0)], axis=0)
        return jnp.concatenate([tall, columns(ref, index, height)], axis=1)

    def coarse_field(m, level):
        return extended(
            wc[m, level], rc_next[m, level], rc_prev[m, level], hyc, m * levels + level
        )

    def fine_field(m, level, main):
        return extended(main, rx_next[m, level], rx_prev[m, level], hy, m * levels + level)

    ends = [
        value.astype(jnp.int32)
        for value in (has[(-1, 0)], has[(1, 0)], has[(0, -1)], has[(0, 1)])
    ]
    for k, value in enumerate(
        stencil_weights(coarse_field(half, 0), coarse_field(half, 1), crows, ccols, *ends)
    ):
        coarse_weights[k] = value

    def coarse_members(j, carry):
        for i in range(batch):
            m = j * batch + i
            for level in range(levels):
                u = apply_passes(coarse_field(m, level), [coarse_weights.at[k] for k in range(5)])
                line[pl.ds(pl.multiple_of((m * levels + level) * crows, 8), crows)] = u[
                    :crows, :ccols
                ]
        return carry

    lax.fori_loop(0, half // batch, coarse_members, 0)
    lanes_out[...] = split_dot(line[pl.ds(0, count)], spread)

    upper = lax.broadcasted_iota(jnp.int32, (2 * RATIO, cols), 0) < RATIO

    def fine_member(m, carry):
        fields = jnp.stack(
            [fine_field(m, level, p_ref[m, level] * d_ref[level]) for level in range(levels)]
        )
        for _ in range(PASSES):
            fields = (
                fine_weights[0][None] * fields
                + fine_weights[1][None] * shift_up(fields, 1)
                + fine_weights[2][None] * shift_down(fields, 1)
                + fine_weights[3][None] * shift_up(fields, 2)
                + fine_weights[4][None] * shift_down(fields, 2)
            )
        for level in range(levels):
            u = fields[level, :rows, :cols]
            base = (m * levels + level) * crows
            for t in range(rows // (2 * RATIO)):
                a = jnp.broadcast_to(lanes_out[pl.ds(base + 2 * t, 1), :], (2 * RATIO, cols))
                b = jnp.broadcast_to(lanes_out[pl.ds(base + 2 * t + 1, 1), :], (2 * RATIO, cols))
                at = slice(2 * RATIO * t, 2 * RATIO * (t + 1))
                acc[level, at] += p_ref[m, level, at] * (u[at] + jnp.where(upper, a, b))
        return carry

    for k, (first, second, low, high) in enumerate(x_moves):
        arrive(first)
        arrive(second)
        if k == 0:
            for j, value in enumerate(
                stencil_weights(
                    fine_field(half, 0, coef_ref[0]), fine_field(half, 1, coef_ref[1]),
                    rows, cols, *ends
                )
            ):
                fine_weights[j] = value
        lax.fori_loop(low, min(high, half), fine_member, 0)

    swap = pltpu.make_async_remote_copy(
        src_ref=acc, dst_ref=acc_other, send_sem=send_sem.at[len(moves)],
        recv_sem=recv_sem.at[len(moves)], device_id={"ma": 1 - ma}, device_id_type=MESH,
    )
    swap.start()
    loads[3].wait()
    swap.wait_recv()
    d, r = d_ref[...], r_ref[...]
    q = d + (acc[...] + acc_other[...]) / (MEMBERS - 1)
    q_ref[...] = q

    def total_row(value):
        flat = value.reshape(levels * rows // 8, 8, cols)
        tile = jnp.sum(flat, axis=0)
        narrow = tile[:, :LANES]
        for k in range(1, cols // LANES):
            narrow = narrow + tile[:, k * LANES : (k + 1) * LANES]
        return jnp.sum(narrow, axis=0, keepdims=True)

    row = lax.broadcasted_iota(jnp.int32, (8, LANES), 0)
    packed = jnp.zeros((8, LANES), F32)
    for k, value in enumerate((r * r, d * q, r * q, q * q)):
        packed = jnp.where(row == k, total_row(value), packed)
    part[...] = packed
    slots[me] = packed

    def to_peer(k):
        return pltpu.make_async_remote_copy(
            src_ref=part, dst_ref=slots.at[me], send_sem=group_send.at[k],
            recv_sem=group_recv.at[me],
            device_id={"gx": k // n_y, "gy": k % n_y}, device_id_type=MESH,
        )

    def from_peer(k):
        return pltpu.make_async_remote_copy(
            src_ref=part, dst_ref=slots.at[k], send_sem=group_send.at[k],
            recv_sem=group_recv.at[k],
            device_id={"gx": k // n_y, "gy": k % n_y}, device_id_type=MESH,
        )

    each_peer(lambda k: to_peer(k).start())
    swap.wait_send()
    for copy, sends, _ in moves:
        @pl.when(sends)
        def _():
            copy.wait_send()
    each_peer(lambda k: from_peer(k).wait_recv())
    sums = jnp.sum(jnp.sum(slots[...], axis=0), axis=1, keepdims=True)
    norm_old, curvature, cross, image = (sums[k : k + 1] for k in range(4))
    step_length = norm_old / curvature
    norm_new = norm_old + step_length * (step_length * image - 2.0 * cross)
    step_ref[...] = jnp.broadcast_to(step_length, (1, cols))
    growth_ref[...] = jnp.broadcast_to(norm_new / norm_old, (1, cols))
    each_peer(lambda k: to_peer(k).wait_send())


def local(n_x, n_y, perturbations, coefficients, coarse_coefficients, iterate, residual, direction):
    half, levels, rows, cols = perturbations.shape
    _, crows, ccols = coarse_coefficients.shape
    total = half + 1
    group = n_x * n_y
    n_moves = 2 * CHUNKS + 2 + 6 + 1
    vmem = pl.BlockSpec(memory_space=pltpu.VMEM)
    q, step_length, growth = pl.pallas_call(
        functools.partial(kernel, (n_x, n_y)),
        out_shape=(
            jax.ShapeDtypeStruct((levels, rows, cols), F32),
            jax.ShapeDtypeStruct((1, cols), F32),
            jax.ShapeDtypeStruct((1, cols), F32),
        ),
        in_specs=[pl.BlockSpec(memory_space=pltpu.HBM)] * 5,
        out_specs=(vmem, vmem, vmem),
        scratch_shapes=[
            pltpu.VMEM((half, levels, rows, cols), F32),
            pltpu.VMEM((2, rows, cols), F32),
            pltpu.VMEM((2, crows, ccols), F32),
            pltpu.VMEM((levels, rows, cols), F32),
            pltpu.VMEM((levels, rows, cols), F32),
            pltpu.VMEM((total, levels, crows, ccols), F32),
            pltpu.VMEM((half * levels * rows, ccols), F32),
            pltpu.VMEM((half * levels * crows, cols), F32),
            pltpu.VMEM((total, levels, HALO, cols), F32),
            pltpu.VMEM((total, levels, HALO, cols), F32),
            pltpu.VMEM((total, levels, HALO, ccols), F32),
            pltpu.VMEM((total, levels, HALO, ccols), F32),
            pltpu.VMEM((2, rows + 2 * crows, LANES), F32),
            pltpu.VMEM((total, levels, HALO, cols), F32),
            pltpu.VMEM((total, levels, HALO, cols), F32),
            pltpu.VMEM((total, levels, HALO, ccols), F32),
            pltpu.VMEM((total, levels, HALO, ccols), F32),
            pltpu.VMEM((2, rows + crows, LANES), F32),
            pltpu.VMEM((2, 2, crows + 8, LANES), F32),
            pltpu.VMEM((2, rows + 2 * HALO, LANES), F32),
            pltpu.VMEM((2, crows + 2 * HALO, LANES), F32),
            pltpu.VMEM((5, rows + 2 * HALO, cols + LANES), F32),
            pltpu.VMEM((5, crows + 2 * HALO, ccols + LANES), F32),
            pltpu.VMEM((levels, rows, cols), F32),
            pltpu.VMEM((levels, rows, cols), F32),
            pltpu.VMEM((8, LANES), F32),
            pltpu.VMEM((group, 8, LANES), F32),
            pltpu.SemaphoreType.DMA((4 + CHUNKS,)),
            pltpu.SemaphoreType.DMA((n_moves,)),
            pltpu.SemaphoreType.DMA((n_moves,)),
            pltpu.SemaphoreType.DMA((group,)),
            pltpu.SemaphoreType.DMA((group,)),
        ],
        compiler_params=pltpu.CompilerParams(
            collective_id=0, has_side_effects=True, vmem_limit_bytes=62 << 20
        ),
    )(perturbations, coefficients, coarse_coefficients, residual, direction)
    new_iterate = iterate + step_length * direction
    new_residual = residual - step_length * q
    new_direction = new_residual + growth * direction
    return (new_iterate, new_residual, new_direction)


def solution(mesh):
    cell = P(None, "gx", "gy")
    return jax.shard_map(
        functools.partial(local, mesh.shape["gx"], mesh.shape["gy"]),
        mesh=mesh,
        in_specs=(P("ma", None, "gx", "gy"), cell, cell, cell, cell, cell),
        out_specs=(cell, cell, cell),
        check_vma=False,
    )
```
